32 devices in a mesh: bin: 4 (over x, core), frame: 8 (over z, y).
Axes of the slice: x: 2, y: 2, z: 4, core: 2. Of those that a mesh axis runs over, the one named last changes fastest.
Arguments:
- signal: bfloat16 [32, 2, 256, 2048], P('bin', None, None, 'frame'), may hold values from -24 to 24
- demix: float32 [32, 256, 512], P('bin'), may hold values from -1 to 2
Outputs:
- demixed: float32 [32, 256, 512], P('bin', 'frame')
- gradient: float32 [32, 256, 512], P('bin', 'frame')
The draws below stay inside these ranges and needn't reach their ends.
All inputs are finite; a program needn't handle non-finite values.
Results may differ from the reference program's by a relative error of at most 0.0061.
Values sent between devices are 32-bit elements; how exact they have to be, the bound alone decides.
A program may use at most 64 MiB of HBM per device.

```python
import math
import jax
import jax.numpy as jnp
from jax import lax

SENSOR_COUNT = 256
BINS = 32
ITERS = 2
TIME_FRAMES = 2048


def draw_signal(key, part):
    root_key, frequency_key, channel_key, pulse_key, frame_key = jax.random.split(jax.random.fold_in(key, 11), 5)
    shape = (BINS, 2, SENSOR_COUNT, TIME_FRAMES)
    root_seed = jnp.clip(jax.random.normal(root_key, shape, jnp.float32), -4.0, 4.0)
    frame_lo, frame_hi = (0.5, 2.0)
    bin_channel = jnp.exp(jax.random.uniform(frequency_key, (BINS, 1, SENSOR_COUNT, 1), jnp.float32, 0.0, math.log(3.0)))
    channel_scale = jnp.exp(jax.random.uniform(channel_key, (1, 1, SENSOR_COUNT, 1), jnp.float32, 0.0, math.log(2.0)))
    pulse_event = jnp.exp(jax.random.uniform(pulse_key, (1, 1, SENSOR_COUNT, TIME_FRAMES), jnp.float32, math.log(0.5), math.log(2.0)))
    frame_factor = jnp.exp(jax.random.uniform(frame_key, (1, 1, 1, TIME_FRAMES), jnp.float32, math.log(frame_lo), math.log(frame_hi)))
    return (0.25 * root_seed * bin_channel * channel_scale * pulse_event * frame_factor).astype(jnp.bfloat16)


def draw_demix(key, part):
    root_key = jax.random.fold_in(key, 23)
    shape = (BINS, SENSOR_COUNT, 2 * SENSOR_COUNT)
    root_seed = jnp.clip(jax.random.normal(root_key, shape, jnp.float32), -4.0, 4.0)
    row_ids = jnp.arange(SENSOR_COUNT).reshape(1, SENSOR_COUNT, 1)
    col_ids = jnp.arange(2 * SENSOR_COUNT).reshape(1, 1, 2 * SENSOR_COUNT)
    identity = jnp.where(row_ids == col_ids, 1.0, 0.0).astype(jnp.float32)
    return identity + 0.5 * root_seed / math.sqrt(SENSOR_COUNT)


def setup_inputs(seed: int = 0) -> dict:
    seeds = jax.random.split(jax.random.key(seed), 3)
    signal = draw_signal(jax.random.fold_in(seeds[2], 71), 0)
    demix = draw_demix(jax.random.fold_in(seeds[2], 71), 0)
    return dict(signal=signal, demix=demix)


step_size = 0.05
small_eps = 1e-06

def complex_matrix(demixing):
    width = demixing.shape[-1] // 2
    real_part = demixing[..., :width]
    imag_part = demixing[..., width:]
    upper = jnp.concatenate([real_part, imag_part], axis=-1)
    lower = jnp.concatenate([-imag_part, real_part], axis=-1)
    return jnp.concatenate([upper, lower], axis=-2)

def stack_signal(spectra):
    real_part = spectra[:, 0]
    imag_part = spectra[:, 1]
    upper = jnp.concatenate([real_part, imag_part], axis=-1)
    lower = jnp.concatenate([-imag_part, real_part], axis=-1)
    return jnp.concatenate([upper, lower], axis=-2)

def reference(signal, demix):
    frame_total = signal.shape[-1]
    demixing = demix
    direction = jnp.zeros_like(demix)
    for iteration in range(ITERS):
        rounded = demixing.astype(jnp.bfloat16)

        def one_bin(pair):
            weights, spectra = pair
            stacked = stack_signal(spectra[None])[0]
            return jnp.dot(weights, stacked, preferred_element_type=jnp.float32)
        sources = lax.map(one_bin, (rounded, signal))
        squares = lax.optimization_barrier(jnp.sum(sources * sources, axis=0))
        power_sum = squares[:, :frame_total] + squares[:, frame_total:]
        radius = jnp.sqrt(power_sum / BINS + small_eps)
        radius_both = jnp.concatenate([radius, radius], axis=1)

        def one_gram(values):
            scored = (values / radius_both).astype(jnp.bfloat16)
            source_b = values.astype(jnp.bfloat16)
            imag_key = jnp.concatenate([-source_b[:, frame_total:], source_b[:, :frame_total]], axis=1)
            dims = (((1,), (1,)), ((), ()))
            real_gram = lax.dot_general(scored, source_b, dims, preferred_element_type=jnp.float32)
            imag_gram = lax.dot_general(scored, imag_key, dims, preferred_element_type=jnp.float32)
            return jnp.concatenate([real_gram, imag_gram], axis=1) / frame_total
        gram_full = lax.map(one_gram, sources)
        product = jnp.einsum('fkj,fjl->fkl', gram_full, complex_matrix(demixing), precision=lax.Precision.HIGHEST)
        direction = demixing - product
        demixing = demixing + step_size * direction
    return (demixing, direction)
```

```python
import functools

import jax
import jax.numpy as jnp
from jax import lax
from jax.experimental import pallas as pl
from jax.experimental.pallas import tpu as pltpu
from jax.sharding import PartitionSpec as P

ITERS = 2

step_size = 0.05
small_eps = 1e-06

MESH = pl.DeviceIdType.MESH
NT = (((1,), (1,)), ((), ()))


def dot(a, b):
    return jnp.dot(a, b, preferred_element_type=jnp.float32)


def dot_nt(a, b):
    return lax.dot_general(a, b, NT, preferred_element_type=jnp.float32)


def kernel(
    group, bin_group, sig, w_in, w_out, d_out,
    flat, w_next, src, gram, ry, part, rz, power, pw_recv, pw_sum, rinv,
    pw_send_sem, pw_recv_sem, y_send, y_recv, z_send, z_recv, ga_send, ga_recv, gy_send, gy_recv,
):
    nb, outer, _, rows, width2 = w_in.shape
    width = width2 // 2
    nt = sig.shape[3]
    total = 2 * outer * rows
    half = total // 2
    frames = nt * group
    bins = nb * bin_group
    me = lax.axis_index("frame")
    mb = lax.axis_index("bin")
    y = lax.rem(me, 2)
    yo = 1 - y
    z = me // 2
    core = lax.rem(mb, 2)
    core_o = 1 - core
    y_dev = {"frame": z * 2 + yo}
    core_dev = {"bin": mb + 1 - 2 * core}
    x_dev = {"bin": lax.rem(mb + 2, bin_group)}
    peers = [{"frame": lax.rem(z + k, outer) * 2 + y} for k in range(1, outer)]

    barrier = pltpu.get_barrier_semaphore()
    for dev in [y_dev, core_dev, x_dev] + peers:
        pl.semaphore_signal(barrier, inc=1, device_id=dev, device_id_type=MESH)
    pl.semaphore_wait(barrier, 3 + len(peers))

    def remote(a, b, s, r, dev):
        return pltpu.make_async_remote_copy(
            src_ref=a, dst_ref=b, send_sem=s, recv_sem=r, device_id=dev, device_id_type=MESH
        )

    def y_copy(it, f):
        return remote(gram.at[it, f, yo], ry.at[it, f], y_send.at[it, f], y_recv.at[it, f], y_dev)

    def z_copy(it, f, k):
        return remote(
            part.at[it, f, lax.rem(z + k, outer)], rz.at[it, f, k - 1],
            z_send.at[it, f], z_recv.at[it, f], peers[k - 1],
        )

    def many(ref, sem):
        return pltpu.make_async_copy(ref, ref, sem)

    def ga_copy(f, k):
        own = w_next.at[f, y, z]
        return remote(own, own, ga_send.at[f], ga_recv.at[f], peers[k - 1])

    def gy_copy(f):
        ref = w_next.at[f, y]
        return remote(ref, ref, gy_send.at[f], gy_recv.at[f], y_dev)

    for it in range(ITERS):
        power[...] = jnp.zeros_like(power)

        def make_sources(f, carry):
            if it > 0:
                other = w_next.at[f, yo]
                remote(other, other, gy_send.at[f], gy_recv.at[f], y_dev).wait_recv()
            for d in range(group):
                if it == 0:
                    block = w_in[f, d // 2, d % 2]
                else:
                    block = w_next[f, d % 2, d // 2]
                flat[f, d * rows:(d + 1) * rows, :] = block
            wr = flat[f, :, :width].astype(jnp.bfloat16)
            wi = flat[f, :, width:].astype(jnp.bfloat16)
            xr = sig[f, 0]
            xi = sig[f, 1]
            yr = dot(wr, xr) - dot(wi, xi)
            yi = dot(wr, xi) + dot(wi, xr)
            src[f, 0] = yr
            src[f, 1] = yi
            power[...] += yr * yr + yi * yi
            return carry

        lax.fori_loop(0, nb, make_sources, 0)

        own_half = pl.ds(pl.multiple_of(core * half, half), half)
        other_half = pl.ds(pl.multiple_of(core_o * half, half), half)
        first = remote(
            power.at[other_half], pw_recv.at[it, 0], pw_send_sem.at[it, 0], pw_recv_sem.at[it, 0], core_dev
        )
        first.start()
        first.wait()
        pw_sum[it, 0] = power[own_half, :] + pw_recv[it, 0]
        second = remote(
            pw_sum.at[it, 0], pw_recv.at[it, 1], pw_send_sem.at[it, 1], pw_recv_sem.at[it, 1], x_dev
        )
        second.start()
        second.wait()
        pw_sum[it, 1] = pw_sum[it, 0] + pw_recv[it, 1]
        third = remote(
            pw_sum.at[it, 1], pw_recv.at[it, 2], pw_send_sem.at[it, 2], pw_recv_sem.at[it, 2], core_dev
        )
        third.start()
        rinv[own_half, :] = 1.0 / jnp.sqrt(pw_sum[it, 1] / bins + small_eps)
        third.wait()
        rinv[other_half, :] = 1.0 / jnp.sqrt(pw_recv[it, 2] / bins + small_eps)

        def make_gram(f, carry):
            inv = rinv[...]
            yr = src[f, 0]
            yi = src[f, 1]
            pr = (yr * inv).astype(jnp.bfloat16)
            pi = (yi * inv).astype(jnp.bfloat16)
            br = yr.astype(jnp.bfloat16)
            bi = yi.astype(jnp.bfloat16)
            real = dot_nt(pr, br) + dot_nt(pi, bi)
            imag = dot_nt(pi, br) - dot_nt(pr, bi)
            for d in range(group):
                gram[it, f, d % 2, d // 2, :, :width] = real[d * rows:(d + 1) * rows]
                gram[it, f, d % 2, d // 2, :, width:] = imag[d * rows:(d + 1) * rows]
            y_copy(it, f).start()
            return carry

        lax.fori_loop(0, nb, make_gram, 0)

        def pair_sum(f):
            y_copy(it, f).wait_recv()
            part[it, f] = gram[it, f, y] + ry[it, f]
            for k in range(1, outer):
                z_copy(it, f, k).start()

        def update(f):
            many(rz.at[it, f], z_recv.at[it, f]).wait()
            acc = part[it, f, z]
            for k in range(outer - 1):
                acc = acc + rz[it, f, k]
            acc = acc * (1.0 / frames)
            w = flat[f]
            a = jnp.dot(acc[:, :width], w, precision=lax.Precision.HIGHEST, preferred_element_type=jnp.float32)
            b = jnp.dot(acc[:, width:], w, precision=lax.Precision.HIGHEST, preferred_element_type=jnp.float32)
            own = w_in[f, z, y] if it == 0 else w_next[f, y, z]
            dr = own[:, :width] - (a[:, :width] - b[:, width:])
            di = own[:, width:] - (a[:, width:] + b[:, :width])
            nr = own[:, :width] + step_size * dr
            ni = own[:, width:] + step_size * di
            if it + 1 < ITERS:
                w_next[f, y, z, :, :width] = nr
                w_next[f, y, z, :, width:] = ni
                for k in range(1, outer):
                    ga_copy(f, k).start()
            else:
                w_out[f, :, :width] = nr
                w_out[f, :, width:] = ni
                d_out[f, :, :width] = dr
                d_out[f, :, width:] = di

        def forward(f):
            others = w_next.at[f, y, pl.ds(0, outer - 1)]
            many(others, ga_recv.at[f]).wait()
            gy_copy(f).start()

        lag_u, lag_f = 2, 4
        last = lag_f if it + 1 < ITERS else lag_u

        def pipeline(s, carry):
            pl.when(s < nb)(lambda: pair_sum(s))
            pl.when(jnp.logical_and(s >= lag_u, s < nb + lag_u))(lambda: update(s - lag_u))
            if it + 1 < ITERS:
                pl.when(s >= lag_f)(lambda: forward(s - lag_f))
            return carry

        lax.fori_loop(0, nb + last, pipeline, 0)

    def drain(f, carry):
        for it in range(ITERS):
            y_copy(it, f).wait_send()
            many(rz.at[it, f], z_send.at[it, f]).wait()
        many(w_next.at[f, y, pl.ds(0, outer - 1)], ga_send.at[f]).wait()
        gy_copy(f).wait_send()
        return carry

    lax.fori_loop(0, nb, drain, 0)


def on_device(signal, demix):
    group = lax.axis_size("frame")
    bin_group = lax.axis_size("bin")
    nb, _, sensors, nt = signal.shape
    total, width2 = demix.shape[1:]
    rows = total // group
    outer = group // 2
    half = total // 2
    f32 = jnp.float32
    out = jax.ShapeDtypeStruct((nb, rows, width2), f32)
    dma = pltpu.SemaphoreType.DMA
    vmem = pl.BlockSpec(memory_space=pltpu.VMEM)
    return pl.pallas_call(
        functools.partial(kernel, group, bin_group),
        out_shape=(out, out),
        in_specs=[vmem, vmem],
        out_specs=(vmem, vmem),
        scratch_shapes=[
            pltpu.VMEM((nb, total, width2), f32),
            pltpu.VMEM((nb, 2, outer, rows, width2), f32),
            pltpu.VMEM((nb, 2, total, nt), f32),
            pltpu.VMEM((ITERS, nb, 2, outer, rows, width2), f32),
            pltpu.VMEM((ITERS, nb, outer, rows, width2), f32),
            pltpu.VMEM((ITERS, nb, outer, rows, width2), f32),
            pltpu.VMEM((ITERS, nb, outer - 1, rows, width2), f32),
            pltpu.VMEM((total, nt), f32),
            pltpu.VMEM((ITERS, 3, half, nt), f32),
            pltpu.VMEM((ITERS, 2, half, nt), f32),
            pltpu.VMEM((total, nt), f32),
            dma((ITERS, 3)),
            dma((ITERS, 3)),
            dma((ITERS, nb)),
            dma((ITERS, nb)),
            dma((ITERS, nb)),
            dma((ITERS, nb)),
            dma((nb,)),
            dma((nb,)),
            dma((nb,)),
            dma((nb,)),
        ],
        compiler_params=pltpu.CompilerParams(
            collective_id=0, has_side_effects=True, vmem_limit_bytes=62 * 1024 * 1024
        ),
    )(signal, demix.reshape(nb, outer, 2, rows, width2))


def solution(mesh):
    placed = (P("bin", None, None, "frame"), P("bin", None, None))
    return jax.shard_map(
        on_device,
        mesh=mesh,
        in_specs=placed,
        out_specs=(P("bin", "frame", None), P("bin", "frame", None)),
        check_vma=False,
    )
```

```python
import functools

import jax
import jax.numpy as jnp
from jax import lax
from jax.experimental import pallas as pl
from jax.experimental.pallas import tpu as pltpu
from jax.sharding import PartitionSpec as P

ITERS = 2
LAGS = (1, 2, 3, 4)

step_size = 0.05
small_eps = 1e-06

MESH = pl.DeviceIdType.MESH
NT = (((1,), (1,)), ((), ()))


def dot(a, b):
    return jnp.dot(a, b, preferred_element_type=jnp.float32)


def dot_nt(a, b):
    return lax.dot_general(a, b, NT, preferred_element_type=jnp.float32)


def kernel(
    group, bin_group, sig, w_in, w_out, d_out,
    flat, w_next, src, gram, r1, part1, r2, part2, r3, power, pw_recv, pw_sum, rinv,
    pw_send_sem, pw_recv_sem, s1_send, s1_recv, s2_send, s2_recv, s3_send, s3_recv,
    g1_send, g1_recv, g2_send, g2_recv, g3_send, g3_recv,
):
    nb, high, _, _, rows, width2 = w_in.shape
    width = width2 // 2
    nt = sig.shape[3]
    total = 4 * high * rows
    half = total // 2
    quarter = total // 4
    frames = nt * group
    bins = nb * bin_group
    me = lax.axis_index("frame")
    mb = lax.axis_index("bin")
    y = lax.rem(me, 2)
    lo = lax.rem(me // 2, 2)
    hi = me // 4
    y_step = 1 - 2 * y
    lo_step = 2 - 4 * lo
    core = lax.rem(mb, 2)
    core_o = 1 - core
    core_dev = {"bin": mb + 1 - 2 * core}
    x_dev = {"bin": lax.rem(mb + 2, bin_group)}
    peers = [{"frame": lax.rem(hi + k, high) * 4 + lax.rem(me, 4)} for k in range(1, high)]

    barrier = pltpu.get_barrier_semaphore()
    for dev in [{"frame": me + y_step}, {"frame": me + lo_step}, core_dev, x_dev] + peers:
        pl.semaphore_signal(barrier, inc=1, device_id=dev, device_id_type=MESH)
    pl.semaphore_wait(barrier, 4 + len(peers))

    def swapped(f):
        return f // (nb - nb // 8)

    def near(f):
        return y + swapped(f) * (lo - y)

    def far(f):
        return lo + swapped(f) * (y - lo)

    def near_dev(f):
        return {"frame": me + y_step + swapped(f) * (lo_step - y_step)}

    def far_dev(f):
        return {"frame": me + lo_step + swapped(f) * (y_step - lo_step)}

    def remote(a, b, s, r, dev):
        return pltpu.make_async_remote_copy(
            src_ref=a, dst_ref=b, send_sem=s, recv_sem=r, device_id=dev, device_id_type=MESH
        )

    def s1_copy(it, f):
        return remote(gram.at[it, f, 1 - near(f)], r1.at[it, f], s1_send.at[it, f], s1_recv.at[it, f], near_dev(f))

    def s2_copy(it, f):
        return remote(part1.at[it, f, 1 - far(f)], r2.at[it, f], s2_send.at[it, f], s2_recv.at[it, f], far_dev(f))

    def s3_copy(it, f, k):
        return remote(
            part2.at[it, f, lax.rem(hi + k, high)], r3.at[it, f, k - 1],
            s3_send.at[it, f], s3_recv.at[it, f], peers[k - 1],
        )

    def many(ref, sem):
        return pltpu.make_async_copy(ref, ref, sem)

    def g3_copy(f, k):
        own = w_next.at[f, near(f), far(f), hi]
        return remote(own, own, g3_send.at[f], g3_recv.at[f], peers[k - 1])

    def g2_copy(f, b):
        ref = w_next.at[f, near(f), b]
        return remote(ref, ref, g2_send.at[f], g2_recv.at[f], far_dev(f))

    def g1_copy(f, a):
        ref = w_next.at[f, a]
        return remote(ref, ref, g1_send.at[f], g1_recv.at[f], near_dev(f))

    for it in range(ITERS):
        power[...] = jnp.zeros_like(power)

        def make_sources(f, carry):
            if it > 0:
                g1_copy(f, 1 - near(f)).wait_recv()
            for d in range(group):
                yd, ld, hd = d % 2, d // 2 % 2, d // 4
                if it == 0:
                    block = w_in[f, hd, ld, yd]
                else:
                    block = w_next[f, yd + swapped(f) * (ld - yd), ld + swapped(f) * (yd - ld), hd]
                q = yd * (group // 2) + d // 2
                flat[f, q * rows:(q + 1) * rows, :] = block
            wr = flat[f, :, :width].astype(jnp.bfloat16)
            wi = flat[f, :, width:].astype(jnp.bfloat16)
            xr = sig[f, 0]
            xi = sig[f, 1]
            yr = dot(wr, xr) - dot(wi, xi)
            yi = dot(wr, xi) + dot(wi, xr)
            src[f, 0] = yr
            src[f, 1] = yi
            power[...] += yr * yr + yi * yi
            return carry

        lax.fori_loop(0, nb, make_sources, 0)

        def piece(parity, which):
            return pl.ds(pl.multiple_of(parity * half + which * quarter, quarter), quarter)

        def exchange(c, step, parity):
            source = power.at[piece(parity, core_o)] if step == 0 else pw_sum.at[it, c, step - 1]
            return remote(
                source, pw_recv.at[it, c, step], pw_send_sem.at[it, c, step],
                pw_recv_sem.at[it, c, step], x_dev if step == 1 else core_dev,
            )

        def add(c, step, parity):
            before = power[piece(parity, core), :] if step == 0 else pw_sum[it, c, step - 1]
            exchange(c, step, parity).wait()
            pw_sum[it, c, step] = before + pw_recv[it, c, step]
            exchange(c, step + 1, parity).start()

        def finish(c, parity):
            rinv[piece(parity, core), :] = 1.0 / jnp.sqrt(pw_sum[it, c, 1] / bins + small_eps)
            exchange(c, 2, parity).wait()
            rinv[piece(parity, core_o), :] = 1.0 / jnp.sqrt(pw_recv[it, c, 2] / bins + small_eps)

        def make_gram(parity, f):
            its_rows = pl.ds(pl.multiple_of(parity * half, half), half)
            inv = rinv[its_rows, :]
            pr = (src[f, 0, its_rows, :] * inv).astype(jnp.bfloat16)
            pi = (src[f, 1, its_rows, :] * inv).astype(jnp.bfloat16)
            br = src[f, 0].astype(jnp.bfloat16)
            bi = src[f, 1].astype(jnp.bfloat16)
            real = dot_nt(pr, br) + dot_nt(pi, bi)
            imag = dot_nt(pi, br) - dot_nt(pr, bi)
            for e in range(group // 2):
                ld, hd = e % 2, e // 2
                na, fa = parity + swapped(f) * (ld - parity), ld + swapped(f) * (parity - ld)
                gram[it, f, na, fa, hd, :, :width] = real[e * rows:(e + 1) * rows]
                gram[it, f, na, fa, hd, :, width:] = imag[e * rows:(e + 1) * rows]

        def away(f, carry):
            make_gram(1 - y, f)
            pl.when(swapped(f) == 0)(lambda: s1_copy(it, f).start())
            return carry

        def kept(f, carry):
            make_gram(y, f)
            pl.when(swapped(f) == 1)(lambda: s1_copy(it, f).start())
            return carry

        exchange(0, 0, 1 - y).start()
        add(0, 0, 1 - y)
        exchange(1, 0, y).start()
        add(0, 1, 1 - y)
        add(1, 0, y)
        finish(0, 1 - y)
        lax.fori_loop(0, nb, away, 0)
        add(1, 1, y)
        finish(1, y)
        lax.fori_loop(0, nb, kept, 0)

        def sum1(f):
            s1_copy(it, f).wait_recv()
            part1[it, f] = gram[it, f, near(f)] + r1[it, f]
            s2_copy(it, f).start()

        def sum2(f):
            s2_copy(it, f).wait_recv()
            part2[it, f] = part1[it, f, far(f)] + r2[it, f]
            for k in range(1, high):
                s3_copy(it, f, k).start()

        def update(f):
            many(r3.at[it, f], s3_recv.at[it, f]).wait()
            acc = part2[it, f, hi]
            for k in range(high - 1):
                acc = acc + r3[it, f, k]
            acc = acc * (1.0 / frames)
            w = flat[f]
            a = jnp.dot(acc[:, :width], w, precision=lax.Precision.HIGHEST, preferred_element_type=jnp.float32)
            b = jnp.dot(acc[:, width:], w, precision=lax.Precision.HIGHEST, preferred_element_type=jnp.float32)
            own = w_in[f, hi, lo, y] if it == 0 else w_next[f, near(f), far(f), hi]
            dr = own[:, :width] - (a[:, :width] - b[:, width:])
            di = own[:, width:] - (a[:, width:] + b[:, :width])
            nr = own[:, :width] + step_size * dr
            ni = own[:, width:] + step_size * di
            if it + 1 < ITERS:
                w_next[f, near(f), far(f), hi, :, :width] = nr
                w_next[f, near(f), far(f), hi, :, width:] = ni
                for k in range(1, high):
                    g3_copy(f, k).start()
            else:
                w_out[f] = own
                d_out[f, :, :width] = dr
                d_out[f, :, width:] = di

        def spread2(f):
            others = w_next.at[f, near(f), far(f), pl.ds(0, high - 1)]
            many(others, g3_recv.at[f]).wait()
            g2_copy(f, far(f)).start()

        def spread1(f):
            g2_copy(f, 1 - far(f)).wait_recv()
            g1_copy(f, near(f)).start()

        stages = [(0, sum1), (LAGS[0], sum2), (LAGS[1], update)]
        if it + 1 < ITERS:
            stages += [(LAGS[2], spread2), (LAGS[3], spread1)]

        def pipeline(s, carry):
            for lag, stage in stages:
                inside = jnp.logical_and(s >= lag, s < nb + lag)
                pl.when(inside)(functools.partial(stage, s - lag))
            return carry

        lax.fori_loop(0, nb + stages[-1][0], pipeline, 0)

    def drain(f, carry):
        for it in range(ITERS):
            s1_copy(it, f).wait_send()
            s2_copy(it, f).wait_send()
            many(r3.at[it, f], s3_send.at[it, f]).wait()
        many(w_next.at[f, near(f), far(f), pl.ds(0, high - 1)], g3_send.at[f]).wait()
        g2_copy(f, far(f)).wait_send()
        g1_copy(f, near(f)).wait_send()
        return carry

    lax.fori_loop(0, nb, drain, 0)


def on_device(signal, demix):
    group = lax.axis_size("frame")
    bin_group = lax.axis_size("bin")
    nb, _, sensors, nt = signal.shape
    total, width2 = demix.shape[1:]
    rows = total // group
    high = group // 4
    quarter = total // 4
    f32 = jnp.float32
    out = jax.ShapeDtypeStruct((nb, rows, width2), f32)
    dma = pltpu.SemaphoreType.DMA
    vmem = pl.BlockSpec(memory_space=pltpu.VMEM)
    own, direction = pl.pallas_call(
        functools.partial(kernel, group, bin_group),
        out_shape=(out, out),
        in_specs=[vmem, vmem],
        out_specs=(vmem, vmem),
        scratch_shapes=[
            pltpu.VMEM((nb, total, width2), f32),
            pltpu.VMEM((nb, 2, 2, high, rows, width2), f32),
            pltpu.VMEM((nb, 2, total, nt), f32),
            pltpu.VMEM((ITERS, nb, 2, 2, high, rows, width2), f32),
            pltpu.VMEM((ITERS, nb, 2, high, rows, width2), f32),
            pltpu.VMEM((ITERS, nb, 2, high, rows, width2), f32),
            pltpu.VMEM((ITERS, nb, high, rows, width2), f32),
            pltpu.VMEM((ITERS, nb, high, rows, width2), f32),
            pltpu.VMEM((ITERS, nb, high - 1, rows, width2), f32),
            pltpu.VMEM((total, nt), f32),
            pltpu.VMEM((ITERS, 2, 3, quarter, nt), f32),
            pltpu.VMEM((ITERS, 2, 2, quarter, nt), f32),
            pltpu.VMEM((total, nt), f32),
            dma((ITERS, 2, 3)),
            dma((ITERS, 2, 3)),
            dma((ITERS, nb)),
            dma((ITERS, nb)),
            dma((ITERS, nb)),
            dma((ITERS, nb)),
            dma((ITERS, nb)),
            dma((ITERS, nb)),
            dma((nb,)),
            dma((nb,)),
            dma((nb,)),
            dma((nb,)),
            dma((nb,)),
            dma((nb,)),
        ],
        compiler_params=pltpu.CompilerParams(
            collective_id=0, has_side_effects=True, vmem_limit_bytes=62 * 1024 * 1024
        ),
    )(signal, demix.reshape(nb, high, 2, 2, rows, width2))
    return own + step_size * direction, direction


def solution(mesh):
    placed = (P("bin", None, None, "frame"), P("bin", None, None))
    return jax.shard_map(
        on_device,
        mesh=mesh,
        in_specs=placed,
        out_specs=(P("bin", "frame", None), P("bin", "frame", None)),
        check_vma=False,
    )
```
